32 devices in a mesh: context: 8 (over z, x), tensor: 4 (over y, core).
Axes of the slice: x: 2, y: 2, z: 4, core: 2. Of those that a mesh axis runs over, the one named last changes fastest.
Arguments:
- queries: bfloat16 [1024, 4096], P('context', 'tensor'), may hold values from -6 to 6
- key_vectors: bfloat16 [1024, 4096], P('context', 'tensor'), may hold values from -6 to 6
- value_vectors: bfloat16 [1024, 4096], P('context', 'tensor'), may hold values from -6 to 6
- doc_lengths: int32 [16], replicated, may hold values from 1 to 256, 1024 in all
- head_gain: float32 [4096], P('tensor'), may hold values from 0.5 to 1.5
- output_weight: bfloat16 [4096, 6144], P('tensor'), may hold values from -0.125 to 0.125
- residual: bfloat16 [1024, 6144], P('context', 'tensor'), may hold values from -6 to 6
- final_gain: float32 [6144], replicated, may hold values from 0.5 to 1.5
Outputs:
- next_stream: bfloat16 [1024, 6144], P('context', 'tensor')
- normed: bfloat16 [1024, 6144], P('context')
The draws below stay inside these ranges and needn't reach their ends.
Inputs may be any that keep to these rules, and one draw needn't show every extreme that they name: `doc_lengths`: the 16 lengths sum to 1024, and one of them equals 256.
All inputs are finite; a program needn't handle non-finite values.
Results may differ from the reference program's by a relative error of at most 0.017.
Values may be sent and summed in bfloat16 or wider, within the bound.
A program may use at most 64 MiB of HBM per device.

```python
import math
import jax
import jax.numpy as jnp
import numpy as np
from jax import lax

D = 6144
HEAD = 128
HEADS = 32
TOK_DEV = 128
DOCS = 16
TOKENS = 1024
MOST = 256
N_CONTEXT = 8
N_TENSOR = 4


def spiked(array, stream_key, source, target, shards_of, factor):
    def block_of(dim):
        return (jnp.arange(array.shape[dim]) // (array.shape[dim] // shards_of)).reshape((-1,) + (1,) * (array.ndim - 1 - dim))

    first = jax.random.permutation(stream_key, shards_of)[block_of(target)]
    far = (block_of(target) + shards_of // 2) % shards_of
    return jnp.where((block_of(source) == first) | (block_of(source) == far), factor * array, array)


def levels(key, dims, shards, smallest, high):
    level, own = 1.0, jax.random.fold_in(key, 6)
    for dim, parts in shards:
        steps = jnp.exp(jax.random.uniform(jax.random.fold_in(own, dim), (parts,), jnp.float32, smallest / len(shards), high / len(shards)))
        level = level * jnp.repeat(steps, dims[dim] // parts).reshape([-1 if axis == dim else 1 for axis in range(len(dims))])
    return level


def profile(number_of, total, limit, skew):
    loads = [(1 << 20) // math.isqrt(rank ** skew) + 1 for rank in range(2, number_of + 1)]
    spare, holding = total - limit - (number_of - 1), [1] * (number_of - 1)
    while spare > 0:
        free = [i for i in range(number_of - 1) if holding[i] < limit]
        whole, left = sum([loads[i] for i in free]), spare
        for i in free:
            more = min(limit - holding[i], max(1, left * loads[i] // whole), spare)
            holding[i] = holding[i] + more
            spare = spare - more
    return np.array([limit] + holding)


def ragged(rng, count, total, limit, lean):
    if count == 2:
        one = jax.random.randint(rng, (), max(1, total - limit), min(limit, total - 1) + 1)
        return jnp.stack([one, total - one])
    sizes = jnp.asarray(profile(count, total, limit, lean), jnp.int32)
    pairs = (count - 1) // 2
    donor, receiver = sizes[1:1 + 2 * pairs:2], sizes[2:2 + 2 * pairs:2]
    slack = jnp.minimum(donor - 1, limit - receiver)
    moved = jax.random.randint(jax.random.fold_in(rng, 1), (pairs,), 0, 1 << 20) % (slack + 1)
    sizes = sizes.at[1:1 + 2 * pairs:2].set(donor - moved).at[2:2 + 2 * pairs:2].set(receiver + moved)
    return sizes[jax.random.permutation(jax.random.fold_in(rng, 2), count)]


def normal_values(own_key, extent, deviation, limit, shards=(), kind=jnp.bfloat16):
    level = levels(own_key, extent, shards, -0.22, 0.18) if shards else 1.0
    array = jax.random.normal(own_key, extent, jnp.float32) * deviation * level
    return jnp.minimum(jnp.maximum(array, -limit), limit).astype(kind)


def noise_with(own_key, dims, width, limit, shards, heavy, kind=jnp.bfloat16):
    drawn = width * jax.random.normal(own_key, dims, jnp.float32)
    if shards:
        drawn = drawn * levels(own_key, dims, shards, -0.22, 0.18)
    return jnp.clip(spiked(drawn, jax.random.fold_in(own_key, 3), *heavy), -limit, limit).astype(kind)


def setup_inputs(seed: int = 0) -> dict:
    seeds = jax.random.split(jax.random.key(seed), 9)
    queries = normal_values(seeds[0], (TOKENS, HEADS * HEAD), 1.0, 6.0, ((0, 8), (1, 4)))
    key_vectors = normal_values(seeds[1], (TOKENS, HEADS * HEAD), 1.0, 6.0, ((0, 8), (1, 4)))
    value_vectors = normal_values(seeds[2], (TOKENS, HEADS * HEAD), 1.0, 6.0, ((0, 8), (1, 4)))
    doc_lengths = ragged(seeds[3], DOCS, TOKENS, MOST, 2).astype(jnp.int32)
    head_gain = jnp.clip(1.0 + 0.1 * jax.random.normal(seeds[4], (HEADS * HEAD,), jnp.float32), 0.5, 1.5)
    output_weight = noise_with(seeds[5], (HEADS * HEAD, D), (HEADS * HEAD) ** -0.5, 0.125, ((0, 4),), (0, 1, 4, 2.0))
    residual = normal_values(seeds[6], (TOKENS, D), 1.0, 6.0, ((0, 8), (1, 4)))
    final_gain = jnp.clip(1.0 + 0.1 * jax.random.normal(seeds[7], (D,), jnp.float32), 0.5, 1.5)
    return dict(queries=queries, key_vectors=key_vectors, value_vectors=value_vectors, doc_lengths=doc_lengths, head_gain=head_gain, output_weight=output_weight, residual=residual, final_gain=final_gain)


EPSILON = 1e-06

def doc_index(positions, starts):
    return lax.optimization_barrier(jnp.sum((positions[:, None] >= starts[None, :]).astype(jnp.int32), axis=1)) - 1

def row_norm(rows, gain):
    squares = lax.optimization_barrier(jnp.mean(rows * rows, axis=-1, keepdims=True))
    return rows * lax.rsqrt(squares + EPSILON) * gain

def reference(queries, key_vectors, value_vectors, doc_lengths, head_gain, output_weight, residual, final_gain):
    starts = jnp.cumsum(doc_lengths) - doc_lengths
    group_width = HEADS // N_TENSOR * HEAD

    def block_step(carry_state, block_idx):
        first_pos = (block_idx * TOK_DEV).astype(jnp.int32)
        query_heads = lax.dynamic_slice_in_dim(queries, first_pos, TOK_DEV, 0).reshape(TOK_DEV, HEADS, HEAD).astype(jnp.float32)
        key_heads = lax.dynamic_slice_in_dim(key_vectors, first_pos, TOK_DEV, 0).reshape(TOK_DEV, HEADS, HEAD).astype(jnp.float32)
        value_heads = lax.dynamic_slice_in_dim(value_vectors, first_pos, TOK_DEV, 0).reshape(TOK_DEV, HEADS, HEAD).astype(jnp.float32)
        positions = first_pos + jnp.arange(TOK_DEV, dtype=jnp.int32)
        doc_ids = doc_index(positions, starts)
        prev_doc = doc_index(jnp.reshape(first_pos - 1, (1,)), starts)[0]
        carry_mask = doc_ids == prev_doc
        last_mask = doc_ids == doc_ids[-1]
        reset_flag = doc_ids[-1] != prev_doc
        scores = jnp.einsum('thd,shd->hts', query_heads, key_heads)
        causal_mask = (positions[None, :] <= positions[:, None]) & (doc_ids[:, None] == doc_ids[None, :])
        weights = jnp.where(causal_mask[None], scores, 0.0).astype(jnp.bfloat16)
        weights = lax.optimization_barrier(weights).astype(jnp.float32)
        inner_term = jnp.einsum('hts,shd->thd', weights, value_heads)
        state_low = lax.optimization_barrier(carry_state.astype(jnp.bfloat16)).astype(jnp.float32)
        cross_term = jnp.einsum('thd,hde->the', query_heads, state_low)
        attention = inner_term + jnp.where(carry_mask[:, None, None], cross_term, 0.0)
        masked_keys = jnp.where(last_mask[:, None, None], key_heads, 0.0)
        local_state = jnp.einsum('thd,the->hde', masked_keys, value_heads)
        new_state = jnp.where(reset_flag, local_state, carry_state + local_state)
        head_out = row_norm(attention, head_gain.reshape(HEADS, HEAD)).astype(jnp.bfloat16).reshape(TOK_DEV, HEADS * HEAD)
        total_sum = jnp.zeros((TOK_DEV, D), jnp.float32)
        for group_idx in range(N_TENSOR):
            lower = group_idx * group_width
            partial_term = jnp.dot(head_out[:, lower:lower + group_width], output_weight[lower:lower + group_width], preferred_element_type=jnp.float32)
            total_sum = total_sum + lax.optimization_barrier(partial_term.astype(jnp.bfloat16)).astype(jnp.float32)
        stream_rows = lax.dynamic_slice_in_dim(residual, first_pos, TOK_DEV, 0).astype(jnp.float32)
        hidden = (stream_rows + total_sum).astype(jnp.bfloat16)
        normed_rows = row_norm(hidden.astype(jnp.float32), final_gain).astype(jnp.bfloat16)
        return (new_state, (hidden, normed_rows))
    initial = jnp.zeros((HEADS, HEAD, HEAD), jnp.float32)
    _, (hidden, normed_rows) = lax.scan(block_step, initial, jnp.arange(N_CONTEXT, dtype=jnp.int32))
    return (hidden.reshape(TOKENS, D), normed_rows.reshape(TOKENS, D))
```

```python
import functools

import jax
import jax.numpy as jnp
from jax import lax
from jax.experimental import pallas as pl
from jax.experimental.pallas import tpu as pltpu
from jax.sharding import PartitionSpec as P

HEAD = 128
EPSILON = 1e-06
DOC_SHARE = 4
SUBS = 3
F32 = jnp.float32
BF16 = jnp.bfloat16


def kernel(
    n_context, n_tensor, reach, doc_count,
    lens, gain, final_gain, q, k, v, res, w_hbm,
    ns_out, nm_out,
    wbuf, st_send, st_recv, st_acc, inner, head_out,
    p_send, p_recv, keep, c_send, c_recv, hid,
    w_sem, st_ss, st_rs, p_ss, p_rs, c_ss, c_rs, g_ss, g_rs, h_ss, h_rs, r_ss, r_rs,
):
    c = lax.axis_index("context")
    t = lax.axis_index("tensor")
    rows = n_tensor // 2
    y, core = t // 2, t % 2
    mate = y * 2 + (1 - core)
    tok, width = q.shape
    heads = width // HEAD
    sub = p_send.shape[-1]
    part = sub * SUBS

    def there(dy):
        return lax.rem(y + dy, rows) if rows > 1 else y

    def back(dy):
        return lax.rem(y - dy + rows, rows) if rows > 1 else y

    def remote(src, dst, ss, rs, context, tensor):
        return pltpu.make_async_remote_copy(
            src_ref=src, dst_ref=dst, send_sem=ss, recv_sem=rs,
            device_id={"context": context, "tensor": tensor},
            device_id_type=pl.DeviceIdType.MESH,
        )

    order = [(dy, s) for s in range(SUBS) for dy in range(1, rows)] + [(0, s) for s in range(SUBS)]
    w_copies = []
    for g, (dy, s) in enumerate(order):
        for mine in range(2):
            owner = there(dy) * 2 + (core if mine else 1 - core)
            col = pl.multiple_of(owner * part + s * sub, 128)
            w_copies.append(
                pltpu.make_async_copy(
                    w_hbm.at[:, pl.ds(col, sub)], wbuf.at[2 * g + mine], w_sem.at[2 * g + mine]
                )
            )

    barrier = pltpu.get_barrier_semaphore()

    def greet(context, tensor):
        pl.semaphore_signal(
            barrier, inc=1, device_id={"context": context, "tensor": tensor},
            device_id_type=pl.DeviceIdType.MESH,
        )

    for j in range(1, reach + 1):
        @pl.when(c >= j)
        def _():
            greet(c - j, t)

        @pl.when(c + j < n_context)
        def _():
            greet(c + j, t)

    greet(c, mate)
    for dy in range(1, rows):
        greet(c, there(dy) * 2 + core)

    for copy in w_copies:
        copy.start()

    starts, total = [], jnp.int32(0)
    for i in range(doc_count):
        starts.append(total)
        total = total + lens[i]

    def doc_of(pos):
        count = jnp.zeros_like(pos) - 1
        for start in starts:
            count = count + (pos >= start).astype(jnp.int32)
        return count

    first = c * tok
    row = lax.broadcasted_iota(jnp.int32, (tok, tok), 0)
    column = lax.broadcasted_iota(jnp.int32, (tok, tok), 1)
    doc_row, doc_col = doc_of(row + first), doc_of(column + first)
    row_h = lax.broadcasted_iota(jnp.int32, (tok, HEAD), 0) + first
    doc_h = doc_of(row_h)
    prev_doc, last_doc = doc_of(first - 1), doc_of(first + tok - 1)
    last_mask = doc_h == last_doc
    carry_mask = doc_h == prev_doc
    causal = (column <= row) & (doc_row == doc_col)

    for h in range(heads):
        cols = slice(h * HEAD, (h + 1) * HEAD)
        masked = jnp.where(last_mask, k[:, cols].astype(F32), 0.0).astype(BF16)
        st_send[:, cols] = lax.dot_general(
            masked, v[:, cols], (((0,), (0,)), ((), ())), preferred_element_type=F32
        ).astype(BF16)

    pl.semaphore_wait(
        barrier, jnp.minimum(c, reach) + jnp.minimum(n_context - 1 - c, reach) + rows
    )

    def state_copy(j, target):
        return remote(st_send, st_recv.at[j - 1], st_ss.at[j - 1], st_rs.at[j - 1], target, t)

    for j in range(1, reach + 1):
        @pl.when(c + j < n_context)
        def _():
            state_copy(j, c + j).start()

    for h in range(heads):
        cols = slice(h * HEAD, (h + 1) * HEAD)
        scores = lax.dot_general(
            q[:, cols], k[:, cols], (((1,), (1,)), ((), ())), preferred_element_type=F32
        )
        weights = jnp.where(causal, scores, 0.0).astype(BF16)
        inner[:, cols] = jnp.dot(weights, v[:, cols], preferred_element_type=F32)

    st_acc[...] = jnp.zeros_like(st_acc)
    for j in range(1, reach + 1):
        same = (doc_of(first - (j - 1) * tok - 1) == prev_doc).astype(F32)

        @pl.when(c >= j)
        def _():
            state_copy(j, c - j).wait_recv()
            st_acc[...] += st_recv[j - 1].astype(F32) * same

    for h in range(heads):
        cols = slice(h * HEAD, (h + 1) * HEAD)
        cross = jnp.dot(q[:, cols], st_acc[:, cols].astype(BF16), preferred_element_type=F32)
        attention = inner[:, cols] + jnp.where(carry_mask, cross, 0.0)
        squares = jnp.mean(attention * attention, axis=-1, keepdims=True)
        head_out[:, cols] = (attention * lax.rsqrt(squares + EPSILON) * gain[:, cols]).astype(BF16)

    def slot(dy, s):
        return dy * SUBS + s

    def mate_copy(dy, s):
        i = slot(dy, s)
        return remote(p_send.at[i], p_recv.at[i], p_ss.at[i], p_rs.at[i], c, mate)

    def cross_copy(dy, s):
        i = slot(dy - 1, s)
        return remote(
            c_send.at[i], c_recv.at[i], c_ss.at[i], c_rs.at[i], c, there(dy) * 2 + core
        )

    def pass_on(dy, s):
        mate_copy(dy, s).wait_recv()
        c_send[slot(dy - 1, s)] = (
            keep[slot(dy, s)] + p_recv[slot(dy, s)].astype(F32)
        ).astype(BF16)
        cross_copy(dy, s).start()

    waiting = None
    for g, (dy, s) in enumerate(order):
        w_copies[2 * g].wait()
        p_send[slot(dy, s)] = jnp.dot(
            head_out[...], wbuf[2 * g], preferred_element_type=F32
        ).astype(BF16)
        mate_copy(dy, s).start()
        w_copies[2 * g + 1].wait()
        keep[slot(dy, s)] = jnp.dot(head_out[...], wbuf[2 * g + 1], preferred_element_type=F32)
        if waiting is not None:
            pass_on(*waiting)
        waiting = (dy, s) if dy else None

    def own_copy(s):
        i = t * SUBS + s
        return remote(hid.at[i], hid.at[i], h_ss.at[s], h_rs.at[s], c, mate)

    def far_copy(dy, s):
        i = slot(dy - 1, s)
        place = t * SUBS + s
        return remote(
            hid.at[place], hid.at[place], g_ss.at[i], g_rs.at[i], c, there(dy) * 2 + core
        )

    def relay_copy(dy, s):
        i = slot(dy - 1, s)
        place = (back(dy) * 2 + core) * SUBS + s
        return remote(hid.at[place], hid.at[place], r_ss.at[i], r_rs.at[i], c, mate)

    def squared(piece):
        rest = 0.0
        x = piece.astype(F32)
        for b in range(0, sub, 128):
            rest = rest + x[:, b : b + 128] * x[:, b : b + 128]
        return rest

    sums = jnp.zeros((tok, 128), F32)
    for s in range(SUBS):
        mate_copy(0, s).wait_recv()
        added = keep[slot(0, s)] + p_recv[slot(0, s)].astype(F32)
        for dy in range(1, rows):
            cross_copy(dy, s).wait_recv()
            added = added + c_recv[slot(dy - 1, s)].astype(F32)
        cols = slice(s * sub, (s + 1) * sub)
        new = (added + res[:, cols].astype(F32)).astype(BF16)
        hid[t * SUBS + s] = new
        for dy in range(1, rows):
            far_copy(dy, s).start()
        own_copy(s).start()
        ns_out[:, cols] = new
        sums = sums + squared(new)

    for s in range(SUBS):
        own_copy(s).wait_recv()
        sums = sums + squared(hid[mate * SUBS + s])
    for s in range(SUBS):
        for dy in range(1, rows):
            far_copy(dy, s).wait_recv()
            relay_copy(dy, s).start()
            sums = sums + squared(hid[(back(dy) * 2 + core) * SUBS + s])
    for s in range(SUBS):
        for dy in range(1, rows):
            relay_copy(dy, s).wait_recv()
            sums = sums + squared(hid[(back(dy) * 2 + 1 - core) * SUBS + s])

    mean = jnp.sum(sums, axis=-1, keepdims=True) * (1.0 / (part * n_tensor))
    scale = lax.rsqrt(mean + EPSILON)
    for i in range(n_tensor * SUBS):
        cols = slice(i * sub, (i + 1) * sub)
        nm_out[:, cols] = (hid[i].astype(F32) * scale * final_gain[:, cols]).astype(BF16)

    for j in range(1, reach + 1):
        @pl.when(c + j < n_context)
        def _():
            state_copy(j, c + j).wait_send()
    for s in range(SUBS):
        own_copy(s).wait_send()
        mate_copy(0, s).wait_send()
        for dy in range(1, rows):
            mate_copy(dy, s).wait_send()
            cross_copy(dy, s).wait_send()
            far_copy(dy, s).wait_send()
            relay_copy(dy, s).wait_send()


def solution(mesh):
    n_context, n_tensor = mesh.shape["context"], mesh.shape["tensor"]

    def local(q, k, v, lens, gain, weight, res, final_gain):
        tok, width = q.shape
        model = weight.shape[1]
        part = model // n_tensor
        sub = part // SUBS
        rows = n_tensor // 2
        longest = tok * n_context // DOC_SHARE
        reach = min(n_context - 1, max(1, -(-longest // tok)))
        pieces = rows * SUBS
        far = max(1, (rows - 1) * SUBS)
        dma = pltpu.SemaphoreType.DMA
        vmem = pl.BlockSpec(memory_space=pltpu.VMEM)
        return pl.pallas_call(
            functools.partial(kernel, n_context, n_tensor, reach, lens.shape[0]),
            name="layer",
            out_shape=(
                jax.ShapeDtypeStruct((tok, part), BF16),
                jax.ShapeDtypeStruct((tok, model), BF16),
            ),
            in_specs=[pl.BlockSpec(memory_space=pltpu.SMEM)] + [vmem] * 6
            + [pl.BlockSpec(memory_space=pl.ANY)],
            out_specs=(vmem, vmem),
            scratch_shapes=[
                pltpu.VMEM((2 * pieces, width, sub), BF16),
                pltpu.VMEM((HEAD, width), BF16),
                pltpu.VMEM((reach, HEAD, width), BF16),
                pltpu.VMEM((HEAD, width), F32),
                pltpu.VMEM((tok, width), F32),
                pltpu.VMEM((tok, width), BF16),
                pltpu.VMEM((pieces, tok, sub), BF16),
                pltpu.VMEM((pieces, tok, sub), BF16),
                pltpu.VMEM((pieces, tok, sub), F32),
                pltpu.VMEM((far, tok, sub), BF16),
                pltpu.VMEM((far, tok, sub), BF16),
                pltpu.VMEM((n_tensor * SUBS, tok, sub), BF16),
                dma((2 * pieces,)),
                dma((reach,)), dma((reach,)),
                dma((pieces,)), dma((pieces,)),
                dma((far,)), dma((far,)),
                dma((far,)), dma((far,)),
                dma((SUBS,)), dma((SUBS,)),
                dma((far,)), dma((far,)),
            ],
            compiler_params=pltpu.CompilerParams(
                collective_id=0, has_side_effects=True, vmem_limit_bytes=60 * 1024 * 1024
            ),
        )(lens, gain.reshape(1, -1), final_gain.reshape(1, -1), q, k, v, res, weight)

    return jax.shard_map(
        local,
        mesh=mesh,
        in_specs=(
            P("context", "tensor"), P("context", "tensor"), P("context", "tensor"), P(),
            P("tensor"), P("tensor", None), P("context", "tensor"), P(),
        ),
        out_specs=(P("context", "tensor"), P("context", None)),
        check_vma=False,
    )
```

```python
import functools

import jax
import jax.numpy as jnp
from jax import lax
from jax.experimental import pallas as pl
from jax.experimental.pallas import tpu as pltpu
from jax.sharding import PartitionSpec as P

HEAD = 128
EPSILON = 1e-06
DOC_SHARE = 4
SUBS = 3
F32 = jnp.float32
BF16 = jnp.bfloat16


def kernel(
    n_context, n_tensor, reach, cuts, relayed, doc_count,
    lens, gain, q, k, v, res, w_hbm,
    ns_out, hid_out, scale_out,
    wbuf, st_send, st_recv, st_acc, inner, head_out,
    p_send, p_recv, keep, c_send, c_recv, hid,
    w_sem, st_ss, st_rs, p_ss, p_rs, c_ss, c_rs, g_ss, g_rs, h_ss, h_rs, r_ss, r_rs, z_ss, o_sem, n_sem,
):
    c = lax.axis_index("context")
    t = lax.axis_index("tensor")
    rows = n_tensor // 2
    y, core = t // 2, t % 2
    mate = y * 2 + (1 - core)
    tok, width = q.shape
    heads = width // HEAD
    sub = p_send.shape[-1]
    part = sub * SUBS

    def there(dy):
        return lax.rem(y + dy, rows) if rows > 1 else y

    def back(dy):
        return lax.rem(y - dy + rows, rows) if rows > 1 else y

    def remote(src, dst, ss, rs, context, tensor):
        return pltpu.make_async_remote_copy(
            src_ref=src, dst_ref=dst, send_sem=ss, recv_sem=rs,
            device_id={"context": context, "tensor": tensor},
            device_id_type=pl.DeviceIdType.MESH,
        )

    order = [(dy, s) for s in range(SUBS) for dy in range(1, rows)] + [(0, s) for s in range(SUBS)]
    w_copies = []
    for g, (dy, s) in enumerate(order):
        for mine in range(2):
            owner = there(dy) * 2 + (core if mine else 1 - core)
            col = pl.multiple_of(owner * part + s * sub, 128)
            w_copies.append(
                pltpu.make_async_copy(
                    w_hbm.at[:, pl.ds(col, sub)], wbuf.at[2 * g + mine], w_sem.at[2 * g + mine]
                )
            )

    barrier = pltpu.get_barrier_semaphore()

    def greet(context, tensor):
        pl.semaphore_signal(
            barrier, inc=1, device_id={"context": context, "tensor": tensor},
            device_id_type=pl.DeviceIdType.MESH,
        )

    for j in range(1, reach + 1):
        @pl.when(c >= j)
        def _():
            greet(c - j, t)

        @pl.when(c + j < n_context)
        def _():
            greet(c + j, t)

    greet(c, mate)
    for dy in range(1, rows):
        greet(c, there(dy) * 2 + core)

    for copy in w_copies:
        copy.start()

    starts, total = [], jnp.int32(0)
    for i in range(doc_count):
        starts.append(total)
        total = total + lens[i]

    def doc_of(pos):
        count = jnp.zeros_like(pos) - 1
        for start in starts:
            count = count + (pos >= start).astype(jnp.int32)
        return count

    first = c * tok
    row = lax.broadcasted_iota(jnp.int32, (tok, tok), 0)
    column = lax.broadcasted_iota(jnp.int32, (tok, tok), 1)
    doc_row, doc_col = doc_of(row + first), doc_of(column + first)
    row_h = lax.broadcasted_iota(jnp.int32, (tok, HEAD), 0) + first
    doc_h = doc_of(row_h)
    prev_doc, last_doc = doc_of(first - 1), doc_of(first + tok - 1)
    last_mask = doc_h == last_doc
    carry_mask = doc_h == prev_doc
    causal = (column <= row) & (doc_row == doc_col)

    each = width // cuts

    def state_copy(j, m, target):
        i = (j - 1) * cuts + m
        return remote(st_send.at[m], st_recv.at[i], st_ss.at[i], st_rs.at[i], target, t)

    def relay_state(m):
        return remote(st_recv.at[cuts + m], st_recv.at[m], z_ss.at[m], st_rs.at[m], c - 1, t)

    def sends(j):
        go = c + j < n_context
        return go & (lax.rem(c, 2) == 0) if relayed and j == 1 else go

    relays = (lax.rem(c, 2) == 1) & (c >= 3)

    for m in range(cuts):
        for h in range(each // HEAD):
            cols = slice(m * each + h * HEAD, m * each + (h + 1) * HEAD)
            masked = jnp.where(last_mask, k[:, cols].astype(F32), 0.0).astype(BF16)
            st_send[m, :, h * HEAD : (h + 1) * HEAD] = lax.dot_general(
                masked, v[:, cols], (((0,), (0,)), ((), ())), preferred_element_type=F32
            ).astype(BF16)
        if m == 0:
            pl.semaphore_wait(
                barrier, jnp.minimum(c, reach) + jnp.minimum(n_context - 1 - c, reach) + rows
            )
        for j in range(reach, 0, -1):
            @pl.when(sends(j))
            def _():
                state_copy(j, m, c + j).start()

    for h in range(heads):
        cols = slice(h * HEAD, (h + 1) * HEAD)
        scores = lax.dot_general(
            q[:, cols], k[:, cols], (((1,), (1,)), ((), ())), preferred_element_type=F32
        )
        weights = jnp.where(causal, scores, 0.0).astype(BF16)
        inner[:, cols] = jnp.dot(weights, v[:, cols], preferred_element_type=F32)

    st_acc[...] = jnp.zeros_like(st_acc)
    for m in range(cuts):
        piece = slice(m * each, (m + 1) * each)
        for j in range(reach, 0, -1):
            same = (doc_of(first - (j - 1) * tok - 1) == prev_doc).astype(F32)

            @pl.when(c >= j)
            def _():
                state_copy(j, m, c - j).wait_recv()
                if relayed and j == 2:
                    @pl.when(relays)
                    def _():
                        relay_state(m).start()
                st_acc[:, piece] += st_recv[(j - 1) * cuts + m].astype(F32) * same

        for h in range(m * each // HEAD, (m + 1) * each // HEAD):
            cols = slice(h * HEAD, (h + 1) * HEAD)
            cross = jnp.dot(q[:, cols], st_acc[:, cols].astype(BF16), preferred_element_type=F32)
            attention = inner[:, cols] + jnp.where(carry_mask, cross, 0.0)
            squares = jnp.mean(attention * attention, axis=-1, keepdims=True)
            head_out[:, cols] = (
                attention * lax.rsqrt(squares + EPSILON) * gain[:, cols]
            ).astype(BF16)

    def slot(dy, s):
        return dy * SUBS + s

    def mate_copy(dy, s):
        i = slot(dy, s)
        return remote(p_send.at[i], p_recv.at[i], p_ss.at[i], p_rs.at[i], c, mate)

    def cross_copy(dy, s):
        i = slot(dy - 1, s)
        return remote(
            c_send.at[i], c_recv.at[i], c_ss.at[i], c_rs.at[i], c, there(dy) * 2 + core
        )

    def pass_on(dy, s):
        mate_copy(dy, s).wait_recv()
        c_send[slot(dy - 1, s)] = (
            keep[slot(dy, s)] + p_recv[slot(dy, s)].astype(F32)
        ).astype(BF16)
        cross_copy(dy, s).start()

    waiting = None
    for g, (dy, s) in enumerate(order):
        w_copies[2 * g].wait()
        p_send[slot(dy, s)] = jnp.dot(
            head_out[...], wbuf[2 * g], preferred_element_type=F32
        ).astype(BF16)
        mate_copy(dy, s).start()
        w_copies[2 * g + 1].wait()
        keep[slot(dy, s)] = jnp.dot(head_out[...], wbuf[2 * g + 1], preferred_element_type=F32)
        if waiting is not None:
            pass_on(*waiting)
        waiting = (dy, s) if dy else None

    def own_copy(s):
        i = t * SUBS + s
        return remote(hid.at[i], hid.at[i], h_ss.at[s], h_rs.at[s], c, mate)

    def far_copy(dy, s):
        i = slot(dy - 1, s)
        place = t * SUBS + s
        return remote(
            hid.at[place], hid.at[place], g_ss.at[i], g_rs.at[i], c, there(dy) * 2 + core
        )

    def relay_copy(dy, s):
        i = slot(dy - 1, s)
        place = (back(dy) * 2 + core) * SUBS + s
        return remote(hid.at[place], hid.at[place], r_ss.at[i], r_rs.at[i], c, mate)

    def squared(piece):
        rest = 0.0
        x = piece.astype(F32)
        for b in range(0, sub, 128):
            rest = rest + x[:, b : b + 128] * x[:, b : b + 128]
        return rest

    def out_copy(i):
        return pltpu.make_async_copy(hid.at[i], hid_out.at[i], o_sem.at[i])

    def stream_copy(s):
        return pltpu.make_async_copy(
            hid.at[t * SUBS + s], ns_out.at[:, pl.ds(s * sub, sub)], n_sem.at[s]
        )

    sums = jnp.zeros((tok, 128), F32)
    for s in range(SUBS):
        mate_copy(0, s).wait_recv()
        added = keep[slot(0, s)] + p_recv[slot(0, s)].astype(F32)
        for dy in range(1, rows):
            cross_copy(dy, s).wait_recv()
            added = added + c_recv[slot(dy - 1, s)].astype(F32)
        cols = slice(s * sub, (s + 1) * sub)
        new = (added + res[:, cols].astype(F32)).astype(BF16)
        hid[t * SUBS + s] = new
        for dy in range(1, rows):
            far_copy(dy, s).start()
        own_copy(s).start()
        stream_copy(s).start()
        out_copy(t * SUBS + s).start()
        sums = sums + squared(new)

    for s in range(SUBS):
        own_copy(s).wait_recv()
        out_copy(mate * SUBS + s).start()
        sums = sums + squared(hid[mate * SUBS + s])
    for s in range(SUBS):
        for dy in range(1, rows):
            far_copy(dy, s).wait_recv()
            relay_copy(dy, s).start()
            out_copy((back(dy) * 2 + core) * SUBS + s).start()
            sums = sums + squared(hid[(back(dy) * 2 + core) * SUBS + s])
    for s in range(SUBS):
        for dy in range(1, rows):
            relay_copy(dy, s).wait_recv()
            out_copy((back(dy) * 2 + 1 - core) * SUBS + s).start()
            sums = sums + squared(hid[(back(dy) * 2 + 1 - core) * SUBS + s])

    mean = jnp.sum(sums, axis=-1, keepdims=True) * (1.0 / (part * n_tensor))
    scale_out[...] = jnp.broadcast_to(lax.rsqrt(mean + EPSILON), (tok, 128))

    for m in range(cuts):
        for j in range(1, reach + 1):
            @pl.when(sends(j))
            def _():
                state_copy(j, m, c + j).wait_send()
        if relayed:
            @pl.when(relays)
            def _():
                relay_state(m).wait_send()
    for i in range(n_tensor * SUBS):
        out_copy(i).wait()
    for s in range(SUBS):
        stream_copy(s).wait()
    for s in range(SUBS):
        own_copy(s).wait_send()
        mate_copy(0, s).wait_send()
        for dy in range(1, rows):
            mate_copy(dy, s).wait_send()
            cross_copy(dy, s).wait_send()
            far_copy(dy, s).wait_send()
            relay_copy(dy, s).wait_send()


def finish(ns, hid, scale, final_gain, ns_out, nm_out):
    sub = hid.shape[-1]

    @pl.when(pl.program_id(0) == 0)
    def _():
        ns_out[...] = ns[...]

    for s in range(SUBS):
        for b in range(0, sub, 128):
            cols = slice(s * sub + b, s * sub + b + 128)
            nm_out[:, cols] = (
                hid[s, :, b : b + 128].astype(F32) * scale[...] * final_gain[:, cols]
            ).astype(BF16)


def solution(mesh):
    n_context, n_tensor = mesh.shape["context"], mesh.shape["tensor"]

    def local(q, k, v, lens, gain, weight, res, final_gain):
        tok, width = q.shape
        model = weight.shape[1]
        part = model // n_tensor
        sub = part // SUBS
        rows = n_tensor // 2
        longest = tok * n_context // DOC_SHARE
        reach = min(n_context - 1, max(1, -(-longest // tok)))
        pieces = rows * SUBS
        far = max(1, (rows - 1) * SUBS)
        relayed = reach == 2 and n_context % 2 == 0
        cuts = 4 if relayed else 1
        count = n_tensor * SUBS
        dma = pltpu.SemaphoreType.DMA
        vmem = pl.BlockSpec(memory_space=pltpu.VMEM)
        ns, hid, scale = pl.pallas_call(
            functools.partial(kernel, n_context, n_tensor, reach, cuts, relayed, lens.shape[0]),
            name="layer",
            out_shape=(
                jax.ShapeDtypeStruct((tok, part), BF16),
                jax.ShapeDtypeStruct((count, tok, sub), BF16),
                jax.ShapeDtypeStruct((tok, 128), F32),
            ),
            in_specs=[pl.BlockSpec(memory_space=pltpu.SMEM)] + [vmem] * 5
            + [pl.BlockSpec(memory_space=pl.ANY)],
            out_specs=(
                pl.BlockSpec(memory_space=pl.ANY), pl.BlockSpec(memory_space=pl.ANY), vmem
            ),
            scratch_shapes=[
                pltpu.VMEM((2 * pieces, width, sub), BF16),
                pltpu.VMEM((cuts, HEAD, width // cuts), BF16),
                pltpu.VMEM((reach * cuts, HEAD, width // cuts), BF16),
                pltpu.VMEM((HEAD, width), F32),
                pltpu.VMEM((tok, width), F32),
                pltpu.VMEM((tok, width), BF16),
                pltpu.VMEM((pieces, tok, sub), BF16),
                pltpu.VMEM((pieces, tok, sub), BF16),
                pltpu.VMEM((pieces, tok, sub), F32),
                pltpu.VMEM((far, tok, sub), BF16),
                pltpu.VMEM((far, tok, sub), BF16),
                pltpu.VMEM((n_tensor * SUBS, tok, sub), BF16),
                dma((2 * pieces,)),
                dma((reach * cuts,)), dma((reach * cuts,)),
                dma((pieces,)), dma((pieces,)),
                dma((far,)), dma((far,)),
                dma((far,)), dma((far,)),
                dma((SUBS,)), dma((SUBS,)),
                dma((far,)), dma((far,)),
                dma((cuts,)), dma((count,)), dma((SUBS,)),
            ],
            compiler_params=pltpu.CompilerParams(
                collective_id=0, has_side_effects=True, vmem_limit_bytes=60 * 1024 * 1024
            ),
        )(lens, gain.reshape(1, -1), q, k, v, res, weight)
        return pl.pallas_call(
            finish,
            name="finish",
            grid=(n_tensor,),
            out_shape=(
                jax.ShapeDtypeStruct((tok, part), BF16),
                jax.ShapeDtypeStruct((tok, model), BF16),
            ),
            in_specs=[
                pl.BlockSpec((tok, part), lambda i: (0, 0)),
                pl.BlockSpec((SUBS, tok, sub), lambda i: (i, 0, 0)),
                pl.BlockSpec((tok, 128), lambda i: (0, 0)),
                pl.BlockSpec((1, part), lambda i: (0, i)),
            ],
            out_specs=(
                pl.BlockSpec((tok, part), lambda i: (0, 0)),
                pl.BlockSpec((tok, part), lambda i: (0, i)),
            ),
        )(ns, hid, scale, final_gain.reshape(1, -1))

    return jax.shard_map(
        local,
        mesh=mesh,
        in_specs=(
            P("context", "tensor"), P("context", "tensor"), P("context", "tensor"), P(),
            P("tensor"), P("tensor", None), P("context", "tensor"), P(),
        ),
        out_specs=(P("context", "tensor"), P("context", None)),
        check_vma=False,
    )
```
